32 devices in a mesh: fsdp: 8 (over z, y), rep: 4 (over x, core).
Axes of the slice: x: 2, y: 2, z: 4, core: 2. Of those that a mesh axis runs over, the one named last changes fastest.
Arguments:
- tokens: bfloat16 [64, 512, 768], P(('fsdp', 'rep')), may hold values from -6 to 6
- page_ids: int32 [64, 512], P(('fsdp', 'rep')), may hold values from 0 to 7, never falling along the last dimension, each value on 1 to 128 neighbouring positions
- box_coords: int32 [8, 64, 512], P(None, ('fsdp', 'rep')), may hold values from 0 to 1000
- w_qkv: bfloat16 [768, 2304], P('fsdp'), may hold values from -0.3125 to 0.3125
- b_qkv: bfloat16 [2304], P('fsdp'), may hold values from -3 to 3
- w_pos: bfloat16 [24576], P('fsdp'), may hold values from -0.75 to 0.75
- w_out: bfloat16 [768, 768], P('fsdp'), may hold values from -0.875 to 0.875
- b_out: bfloat16 [768], P('fsdp'), may hold values from -3 to 3
- gain_one: bfloat16 [768], P('fsdp'), may hold values from 0.5 to 1.5
- shift_one: bfloat16 [768], P('fsdp'), may hold values from -3 to 3
- w_up: bfloat16 [768, 3072], P('fsdp'), may hold values from -0.21875 to 0.21875
- b_up: bfloat16 [3072], P('fsdp'), may hold values from -3 to 3
- w_down: bfloat16 [3072, 768], P('fsdp'), may hold values from -0.109375 to 0.109375
- b_down: bfloat16 [768], P('fsdp'), may hold values from -3 to 3
- gain_two: bfloat16 [768], P('fsdp'), may hold values from 0.5 to 1.5
- shift_two: bfloat16 [768], P('fsdp'), may hold values from -3 to 3
- cotangent: bfloat16 [64, 512, 768], P(('fsdp', 'rep')), may hold values from -6 to 6
Outputs:
- layer_out: bfloat16 [64, 512, 768], P(('fsdp', 'rep'))
- grad_tokens: bfloat16 [64, 512, 768], P(('fsdp', 'rep'))
- grad_w_qkv: float32 [768, 2304], P('fsdp')
- grad_b_qkv: float32 [2304], P('fsdp')
- grad_w_pos: float32 [24576], P('fsdp')
- grad_w_out: float32 [768, 768], P('fsdp')
- grad_b_out: float32 [768], P('fsdp')
- grad_gain_one: float32 [768], P('fsdp')
- grad_shift_one: float32 [768], P('fsdp')
- grad_w_up: float32 [768, 3072], P('fsdp')
- grad_b_up: float32 [3072], P('fsdp')
- grad_w_down: float32 [3072, 768], P('fsdp')
- grad_b_down: float32 [768], P('fsdp')
- grad_gain_two: float32 [768], P('fsdp')
- grad_shift_two: float32 [768], P('fsdp')
The draws below stay inside these ranges and needn't reach their ends.
Inputs may be any that keep to these rules, and one draw needn't show every extreme that they name: `page_ids`: within a row page ids never fall; every page holds 1 to 128 tokens, and one page of every row exactly 128.
All inputs are finite; a program needn't handle non-finite values.
Results may differ from the reference program's by a relative error of at most 0.017.
Values may be sent and summed in bfloat16 or wider, within the bound.
No kernel may reach another device: no remote copies, remote signals or barrier semaphores. Data moves between devices by JAX's collectives and lax.ppermute only.
A program may use at most 256 MiB of HBM per device.

```python
import math
from functools import partial
import jax
import jax.numpy as jnp
import numpy as np
from jax import lax

D = 768
HEADS = 12
HD = 64
FF = 3072
PE = 192
L = 512
PAGES = 8
MOST = 128
ROWS = 64


def plant(array, stream_key, least, high):
    index_at = [jax.random.randint(jax.random.fold_in(stream_key, axis), (), 0, length) for axis, length in enumerate(array.shape)]
    longest = array.shape.index(max(array.shape))
    next_to = index_at[:longest] + [(index_at[longest] + 1) % array.shape[longest]] + index_at[longest + 1:]
    return array.at[tuple(index_at)].set(least).at[tuple(next_to)].set(high)


def raised(drawn, own_key, source, target, blocks, factor):
    def block_of(position):
        return (jnp.arange(drawn.shape[position]) // (drawn.shape[position] // blocks)).reshape((-1,) + (1,) * (drawn.ndim - 1 - position))

    one_side = jax.random.permutation(own_key, blocks)[block_of(target)]
    second = (block_of(target) + blocks // 2) % blocks
    return jnp.where((block_of(source) == one_side) | (block_of(source) == second), factor * drawn, drawn)


def levels(rng, shape, shards, low, high):
    level, own = 1.0, jax.random.fold_in(rng, 6)
    for axis_at, blocks in shards:
        heights = jnp.exp(jax.random.uniform(jax.random.fold_in(own, axis_at), (blocks,), jnp.float32, low / len(shards), high / len(shards)))
        level = level * jnp.repeat(heights, shape[axis_at] // blocks).reshape([-1 if axis == axis_at else 1 for axis in range(len(shape))])
    return level


def split_up(amount, total, bound, skew):
    portions = [(1 << 20) // math.isqrt(grade ** skew) + 1 for grade in range(2, amount + 1)]
    rest, holding = total - bound - (amount - 1), [1] * (amount - 1)
    while rest > 0:
        candidates = [i for i in range(amount - 1) if holding[i] < bound]
        pool, budget = sum([portions[i] for i in candidates]), rest
        for i in candidates:
            more = min(bound - holding[i], max(1, budget * portions[i] // pool), rest)
            holding[i] = holding[i] + more
            rest = rest - more
    return np.array([bound] + holding)


def ragged_sizes(key, amount, total, limit, slope):
    if amount == 2:
        one = jax.random.randint(key, (), max(1, total - limit), min(limit, total - 1) + 1)
        return jnp.stack([one, total - one])
    sizes = jnp.asarray(split_up(amount, total, limit, slope), jnp.int32)
    twos = (amount - 1) // 2
    giver, sink = sizes[1:1 + 2 * twos:2], sizes[2:2 + 2 * twos:2]
    room = jnp.minimum(giver - 1, limit - sink)
    moved = jax.random.randint(jax.random.fold_in(key, 1), (twos,), 0, 1 << 20) % (room + 1)
    sizes = sizes.at[1:1 + 2 * twos:2].set(giver - moved).at[2:2 + 2 * twos:2].set(sink + moved)
    return sizes[jax.random.permutation(jax.random.fold_in(key, 2), amount)]


def scatter_about(stream_key, extent, scale, bound, split=(), kind=jnp.bfloat16):
    level = levels(stream_key, extent, split, -0.22, 0.18) if split else 1.0
    entries = jax.random.normal(stream_key, extent, jnp.float32) * scale * level
    return jnp.minimum(jnp.maximum(entries, -bound), bound).astype(kind)


def gaussian_with(own_key, dims, deviation, bound, pieces, heavy, held_as=jnp.bfloat16):
    entries = deviation * jax.random.normal(own_key, dims, jnp.float32)
    if pieces:
        entries = entries * levels(own_key, dims, pieces, -0.22, 0.18)
    return jnp.clip(raised(entries, jax.random.fold_in(own_key, 3), *heavy), -bound, bound).astype(held_as)


def setup_inputs(seed: int = 0) -> dict:
    seeds = jax.random.split(jax.random.key(seed), 18)
    tokens = scatter_about(seeds[0], (ROWS, L, D), 1.0, 6.0, ((0, 32),))
    page_ids = jax.vmap(lambda own: jnp.searchsorted(jnp.cumsum(ragged_sizes(own, PAGES, L, MOST, 2)), jnp.arange(L), side="right"))(jax.random.split(seeds[1], ROWS)).reshape((ROWS, L)).astype(jnp.int32)
    box_coords = plant(jax.random.randint(seeds[2], (8, ROWS, L), 0, 1001), jax.random.fold_in(seeds[2], 1), 0, 1000).astype(jnp.int32)
    w_qkv = scatter_about(seeds[3], (D, 3 * D), (D // 2) ** -0.5, 0.3125, ((0, 8),))
    b_qkv = scatter_about(seeds[4], (3 * D,), 0.3, 3.0, ((0, 8),))
    w_pos = scatter_about(seeds[5], (2 * PE * HD,), HD ** -0.5, 0.75, ((0, 8),))
    w_out = scatter_about(seeds[6], (D, D), (D // 16) ** -0.5, 0.875, ((0, 8),))
    b_out = scatter_about(seeds[7], (D,), 0.3, 3.0, ((0, 8),))
    gain_one = jnp.clip(1.0 + 0.1 * jax.random.normal(seeds[8], (D,), jnp.float32), 0.5, 1.5).astype(jnp.bfloat16)
    shift_one = scatter_about(seeds[9], (D,), 0.3, 3.0, ((0, 8),))
    w_up = scatter_about(seeds[10], (D, FF), D ** -0.5, 0.21875, ((0, 8),))
    b_up = scatter_about(seeds[11], (FF,), 0.3, 3.0, ((0, 8),))
    w_down = scatter_about(seeds[12], (FF, D), FF ** -0.5, 0.109375, ((0, 8),))
    b_down = scatter_about(seeds[13], (D,), 0.3, 3.0, ((0, 8),))
    gain_two = jnp.clip(1.0 + 0.1 * jax.random.normal(seeds[14], (D,), jnp.float32), 0.5, 1.5).astype(jnp.bfloat16)
    shift_two = scatter_about(seeds[15], (D,), 0.3, 3.0, ((0, 8),))
    cotangent = gaussian_with(seeds[16], (ROWS, L, D), 1.0, 6.0, ((0, 32),), (0, 2, 32, 2.75))
    return {"tokens": tokens, "page_ids": page_ids, "box_coords": box_coords, "w_qkv": w_qkv, "b_qkv": b_qkv, "w_pos": w_pos, "w_out": w_out, "b_out": b_out, "gain_one": gain_one, "shift_one": shift_one, "w_up": w_up, "b_up": b_up, "w_down": w_down, "b_down": b_down, "gain_two": gain_two, "shift_two": shift_two, "cotangent": cotangent}


@jax.custom_vjp
def low(v):
    return lax.optimization_barrier(v.astype(jnp.bfloat16)).astype(jnp.float32)

@jax.custom_vjp
def low_back(v):
    return v

def low_keep(v):
    return (low(v), None)

def low_pass(kept, grad):
    return (grad,)

def back_keep(v):
    return (v, None)

def back_low(kept, grad):
    return (low(grad),)
low.defvjp(low_keep, low_pass)
low_back.defvjp(back_keep, back_low)
norm_eps = 1e-12

def matmul(left_mat, right_mat):
    return jnp.dot(left_mat, right_mat, precision=lax.Precision.HIGHEST)

def layer_norm(values, gain, shift):
    center = lax.optimization_barrier(jnp.mean(values, axis=-1, keepdims=True))
    offset = values - center
    spread = lax.optimization_barrier(jnp.mean(offset * offset, axis=-1, keepdims=True))
    return offset * lax.rsqrt(spread + norm_eps) * gain + shift

def box_features(box_coords):
    freq_count = PE // 16
    freq_vals = jnp.exp(jnp.arange(freq_count).astype(jnp.float32) * (-math.log(10000.0) / freq_count))
    angles = jnp.moveaxis(box_coords, 0, -1).astype(jnp.float32)[..., None] * freq_vals
    stacked = jnp.stack([jnp.sin(angles), jnp.cos(angles)], axis=-1)
    return stacked.reshape(angles.shape[:-2] + (PE,))

def rotate(avec, box_feats):
    pair_vals = avec.reshape(avec.shape[:-1] + (avec.shape[-1] // 2, 2))
    angle_vals = box_feats.reshape(box_feats.shape[:-1] + (box_feats.shape[-1] // 2, 2))
    sin_slot = pair_vals[..., 1] * angle_vals[..., 0] - pair_vals[..., 0] * angle_vals[..., 1]
    cos_slot = pair_vals[..., 0] * angle_vals[..., 0] + pair_vals[..., 1] * angle_vals[..., 1]
    return jnp.stack([sin_slot, cos_slot], axis=-1).reshape(avec.shape)

def attend(score_scale, inputs):
    left_side, right_side, value_heads, row_pages = inputs
    logits = low_back(jnp.einsum('ihe,jhe->hij', left_side, right_side, precision=lax.Precision.HIGHEST))
    same_page = row_pages[:, None] == row_pages[None, :]
    scores = jnp.where(same_page[None], logits * score_scale, -1e+30)
    row_max = lax.optimization_barrier(jnp.max(scores, axis=-1, keepdims=True))
    expo_vals = jnp.exp(scores - row_max)
    attn_probs = low(expo_vals / lax.optimization_barrier(jnp.sum(expo_vals, axis=-1, keepdims=True)))
    return jnp.einsum('hij,jhd->ihd', attn_probs, value_heads, precision=lax.Precision.HIGHEST)

def block(flat_rows, params, box_feats, page_ids):
    w_qkv, b_qkv, w_pos, w_out, b_out, gain_one, shift_one, w_up, b_up, w_down, b_down, gain_two, shift_two = params
    row_count, seq_len = page_ids.shape
    tok_count, model_width = flat_rows.shape
    qkv_sum = low_back(low(matmul(flat_rows, w_qkv) + b_qkv))
    query_heads = qkv_sum[:, :model_width].reshape(tok_count, HEADS, HD)
    key_heads = qkv_sum[:, model_width:2 * model_width].reshape(tok_count, HEADS, HD)
    value_heads = qkv_sum[:, 2 * model_width:].reshape(tok_count, HEADS, HD)
    pos_all = w_pos.reshape(2, PE, HD)
    query_pos = jnp.einsum('nhd,fd->nhf', query_heads, pos_all[1], precision=lax.Precision.HIGHEST)
    key_pos = jnp.einsum('nhd,fd->nhf', key_heads, pos_all[0], precision=lax.Precision.HIGHEST)
    turned_query = low(rotate(query_pos, box_feats))
    turned_key = low(rotate(key_pos, box_feats))
    feats_heads = jnp.broadcast_to(low(box_feats), (tok_count, HEADS, PE))
    left_all = jnp.concatenate([query_heads, turned_query, feats_heads], axis=-1)
    right_all = jnp.concatenate([key_heads, feats_heads, turned_key], axis=-1)

    def by_rows(array_in):
        return array_in.reshape((row_count, seq_len) + array_in.shape[1:])
    ctx_rows = lax.map(jax.checkpoint(partial(attend, 1.0 / math.sqrt(HD + 2 * PE))), (by_rows(left_all), by_rows(right_all), by_rows(value_heads), page_ids))
    ctx_all = low_back(low(ctx_rows.reshape(tok_count, model_width)))
    attn_out = low_back(matmul(ctx_all, w_out) + b_out)
    hidden = layer_norm(flat_rows + attn_out, gain_one, shift_one)
    up_proj = low_back(matmul(low(hidden), w_up) + b_up)
    activated = low(jax.nn.gelu(up_proj, approximate=False))
    ffn_out = low_back(matmul(activated, w_down) + b_down)
    return layer_norm(hidden + ffn_out, gain_two, shift_two)

def reference(tokens, page_ids, box_coords, w_qkv, b_qkv, w_pos, w_out, b_out, gain_one, shift_one, w_up, b_up, w_down, b_down, gain_two, shift_two, cotangent):
    row_count, seq_len, model_width = tokens.shape
    tok_count = row_count * seq_len
    box_feats = box_features(box_coords).reshape(tok_count, 1, PE)
    params = (w_qkv.astype(jnp.float32), b_qkv.astype(jnp.float32), w_pos.astype(jnp.float32), w_out.astype(jnp.float32), b_out.astype(jnp.float32), gain_one.astype(jnp.float32), shift_one.astype(jnp.float32), w_up.astype(jnp.float32), b_up.astype(jnp.float32), w_down.astype(jnp.float32), b_down.astype(jnp.float32), gain_two.astype(jnp.float32), shift_two.astype(jnp.float32))
    flat_rows = tokens.reshape(tok_count, model_width).astype(jnp.float32)

    def forward(flat_in, *weights):
        return block(flat_in, weights, box_feats, page_ids)
    result, pullback = jax.vjp(forward, flat_rows, *params)
    grads = pullback(cotangent.reshape(tok_count, model_width).astype(jnp.float32))
    layer_out = result.reshape(row_count, seq_len, model_width).astype(jnp.bfloat16)
    grad_tokens = grads[0].reshape(row_count, seq_len, model_width).astype(jnp.bfloat16)
    return (layer_out, grad_tokens, grads[1], grads[2], grads[3], grads[4], grads[5], grads[6], grads[7], grads[8], grads[9], grads[10], grads[11], grads[12], grads[13])
```

```python
import math

import jax
import jax.numpy as jnp
from jax import lax
from jax.experimental import pallas as pl
from jax.experimental.pallas import tpu as pltpu
from jax.sharding import PartitionSpec as P

HEADS = 12
HD = 64
PE = 192
LANES = 128
SCALE = 1.0 / math.sqrt(HD + 2 * PE)


norm_eps = 1e-12


def comb_weights(pos):
    pairs = pos.reshape(PE // 2, 2, HD)
    eye = jnp.eye(HD, dtype=pos.dtype)
    one = jnp.concatenate(
        [pairs[:, 0].T, eye[:, : HD // 2], pairs[:, 1].T, eye[:, HD // 2 :]], axis=1
    )
    none = jnp.zeros_like(one)
    return jnp.stack(
        [jnp.concatenate([one, none], axis=0), jnp.concatenate([none, one], axis=0)]
    )


def features(box_coords):
    coords = jnp.moveaxis(box_coords, 0, -1).reshape(-1, 8).astype(jnp.float32)
    freq_count = PE // 16
    freq_vals = jnp.exp(
        jnp.arange(freq_count).astype(jnp.float32) * (-math.log(10000.0) / freq_count)
    )
    angles = (coords[:, :, None] * freq_vals).reshape(coords.shape[0], PE // 2)
    spare = ((0, 0), (0, LANES - PE // 2))
    sines, cosines = jnp.sin(angles), jnp.cos(angles)
    return (
        jnp.pad(sines, spare),
        jnp.pad(-cosines, spare, constant_values=1.0),
        jnp.pad(cosines, spare, constant_values=1.0),
    )


def mm(a, b):
    return lax.dot_general(a, b, (((1,), (0,)), ((), ())), preferred_element_type=jnp.float32)


def mm_nt(a, b):
    return lax.dot_general(a, b, (((1,), (1,)), ((), ())), preferred_element_type=jnp.float32)


def mm_tn(a, b):
    return lax.dot_general(a, b, (((0,), (0,)), ((), ())), preferred_element_type=jnp.float32)


def spare_lanes(shape):
    return lax.broadcasted_iota(jnp.int32, shape, 1) >= PE // 2


def attend_kernel(
    x_ref, wq_ref, wk_ref, wv_ref, bq_ref, bk_ref, bv_ref, cq_ref, ck_ref,
    sn_ref, cn_ref, cp_ref, pc_ref, pr_ref,
    q_out, k_out, v_out, ctx_out, p_out, bias_ref,
):
    pair, row = pl.program_id(0), pl.program_id(1)

    @pl.when(pair == 0)
    def _():
        for b in range(2):
            same = pc_ref[pl.ds(256 * b, 256), :] == pr_ref[0, :, pl.ds(128 * b, 384)]
            bias_ref[row, b] = jnp.where(same, 0.0, -1e30)

    weights = jnp.concatenate([wq_ref[...], wk_ref[...], wv_ref[...]], axis=1)
    biases = jnp.concatenate([bq_ref[...], bk_ref[...], bv_ref[...]], axis=1)
    qkv = (mm(x_ref[...], weights) + biases.astype(jnp.float32)).astype(jnp.bfloat16)
    q, k, v = qkv[:, :LANES], qkv[:, LANES : 2 * LANES], qkv[:, 2 * LANES :]
    q_out[...] = q
    k_out[...] = k
    v_out[...] = v
    sn, cn, cp = sn_ref[...], cn_ref[...], cp_ref[...]
    spare = spare_lanes(sn.shape)
    sin_low = sn.astype(jnp.bfloat16)
    cos_low = jnp.where(spare, 0.0, cp).astype(jnp.bfloat16)
    parts = []
    for e in range(2):
        oq, ok = mm(q, cq_ref[e]), mm(k, ck_ref[e])
        q0, q1 = oq[:, :LANES], oq[:, LANES:]
        k0, k1 = ok[:, :LANES], ok[:, LANES:]
        lq0 = (q0 * cn + q1 * sn).astype(jnp.bfloat16)
        lq1 = (q0 * sn + q1 * cp).astype(jnp.bfloat16)
        lk0 = (k0 * cn + k1 * sn).astype(jnp.bfloat16)
        lk1 = (k0 * sn + k1 * cp).astype(jnp.bfloat16)
        m0 = jnp.where(spare, lk0, sin_low)
        m1 = jnp.where(spare, lk1, cos_low)
        left = jnp.concatenate([lq0, lq1, sin_low, cos_low], axis=1)
        right = jnp.concatenate([m0, m1, lk0, lk1], axis=1)
        halves = []
        for b in range(2):
            s = mm_nt(left[256 * b : 256 * b + 256], right[128 * b : 128 * b + 384])
            s = s * SCALE + bias_ref[row, b]
            s = jnp.exp(s - jnp.max(s, axis=1, keepdims=True))
            p = (s * (1.0 / jnp.sum(s, axis=1, keepdims=True))).astype(jnp.bfloat16)
            p_out[0, e, b] = p
            halves.append(mm(p, v[128 * b : 128 * b + 384]))
        parts.append(jnp.concatenate(halves, axis=0))
    first = lax.broadcasted_iota(jnp.int32, parts[0].shape, 1) < HD
    ctx_out[...] = jnp.where(first, parts[0], parts[1]).astype(jnp.bfloat16)


def attend(x, w_qkv, b_qkv, comb_q, comb_k, feats, page_ids):
    tokens, width = x.shape
    rows, length = page_ids.shape
    pairs = width // LANES
    row_block = lambda w: pl.BlockSpec((length, w), lambda p, r: (r, 0))
    pair_block = pl.BlockSpec((length, LANES), lambda p, r: (r, p))
    weight = lambda at: pl.BlockSpec((width, LANES), lambda p, r: (0, at * pairs + p))
    bias = lambda at: pl.BlockSpec((1, LANES), lambda p, r: (0, at * pairs + p))
    whole = lambda s: pl.BlockSpec(s, lambda p, r: (0,) * len(s))
    slab = jax.ShapeDtypeStruct((tokens, width), jnp.bfloat16)
    b2 = b_qkv.reshape(1, -1)
    return pl.pallas_call(
        attend_kernel,
        name="attend",
        grid=(pairs, rows),
        in_specs=[
            row_block(width), weight(0), weight(1), weight(2), bias(0), bias(1), bias(2),
            whole(comb_q.shape), whole(comb_k.shape),
            row_block(LANES), row_block(LANES), row_block(LANES),
            row_block(1), pl.BlockSpec((1, 1, length), lambda p, r: (r, 0, 0)),
        ],
        out_specs=[
            pair_block, pair_block, pair_block, pair_block,
            pl.BlockSpec((1, 2, 2, 256, 384), lambda p, r: (r, p, 0, 0, 0)),
        ],
        out_shape=[slab, slab, slab, slab,
                   jax.ShapeDtypeStruct((rows, 2 * pairs, 2, 256, 384), jnp.bfloat16)],
        scratch_shapes=[pltpu.VMEM((rows, 2, 256, 384), jnp.float32)],
        compiler_params=pltpu.CompilerParams(vmem_limit_bytes=48 << 20),
    )(x, w_qkv, w_qkv, w_qkv, b2, b2, b2, comb_q, comb_k, *feats,
      page_ids.reshape(tokens, 1), page_ids.reshape(rows, 1, length))


def attend_back_kernel(
    q_ref, k_ref, v_ref, p_ref, dctx_ref, cq_ref, ck_ref, sn_ref, cn_ref, cp_ref,
    dq_out, dk_out, dv_out, gp_out,
):
    @pl.when((pl.program_id(0) == 0) & (pl.program_id(1) == 0))
    def _():
        gp_out[...] = jnp.zeros_like(gp_out)

    q, k, v, dctx = q_ref[...], k_ref[...], v_ref[...], dctx_ref[...]
    sn, cn, cp = sn_ref[...], cn_ref[...], cp_ref[...]
    spare = spare_lanes(sn.shape)
    sin_low = sn.astype(jnp.bfloat16)
    cos_low = jnp.where(spare, 0.0, cp).astype(jnp.bfloat16)
    first = lax.broadcasted_iota(jnp.int32, q.shape, 1) < HD
    dq = dk = None
    dvs = []
    for e in range(2):
        mine = first if e == 0 else ~first
        oq, ok = mm(q, cq_ref[e]).astype(jnp.bfloat16), mm(k, ck_ref[e]).astype(jnp.bfloat16)
        mix_q = jnp.concatenate(
            [jnp.where(spare, oq[:, :LANES], sin_low), jnp.where(spare, oq[:, LANES:], cos_low)], axis=1
        )
        mix_k = jnp.concatenate(
            [jnp.where(spare, ok[:, :LANES], sin_low), jnp.where(spare, ok[:, LANES:], cos_low)], axis=1
        )
        dc = jnp.where(mine, dctx, jnp.zeros_like(dctx))
        dleft, dright, dval = [], [], []
        for b in range(2):
            qs, ks = slice(256 * b, 256 * b + 256), slice(128 * b, 128 * b + 384)
            p_low = p_ref[0, e, b]
            p = p_low.astype(jnp.float32)
            dp = mm_nt(dc[qs], v[ks])
            inner = jnp.sum(dp * p, axis=1, keepdims=True)
            dt = (p * (dp - inner) * SCALE).astype(jnp.bfloat16)
            dleft.append(mm(dt, mix_k[ks]))
            dright.append(mm_tn(dt, mix_q[qs]))
            dval.append(mm_tn(p_low, dctx[qs]))
        dl = jnp.concatenate(dleft, axis=0)

        def joined(pieces):
            a, c = pieces
            return jnp.concatenate([a[:128], a[128:] + c[:256], c[256:]], axis=0)

        dr = joined(dright)
        dvs.append(joined(dval))
        for side, grad in (("q", dl), ("k", dr)):
            g0, g1 = grad[:, :LANES], grad[:, LANES:]
            turned = jnp.concatenate([g0 * cn + g1 * sn, g0 * sn + g1 * cp], axis=1).astype(jnp.bfloat16)
            if side == "q":
                part = mm_nt(turned, cq_ref[e])
                dq = part if dq is None else dq + part
                gp_out[1, e] += mm_tn(q, turned)
            else:
                part = mm_nt(turned, ck_ref[e])
                dk = part if dk is None else dk + part
                gp_out[0, e] += mm_tn(k, turned)
    dq_out[...] = dq.astype(jnp.bfloat16)
    dk_out[...] = dk.astype(jnp.bfloat16)
    dv_out[...] = jnp.where(first, dvs[0], dvs[1]).astype(jnp.bfloat16)


def attend_back(q, k, v, probs, dctx, comb_q, comb_k, feats):
    tokens, width = q.shape
    rows = probs.shape[0]
    length = tokens // rows
    pairs = width // LANES
    row_block = lambda w: pl.BlockSpec((length, w), lambda p, r: (r, 0))
    pair_block = pl.BlockSpec((length, LANES), lambda p, r: (r, p))
    whole = lambda s: pl.BlockSpec(s, lambda p, r: (0,) * len(s))
    slab = jax.ShapeDtypeStruct((tokens, width), jnp.bfloat16)
    gp_shape = (2, 2, LANES, 2 * LANES)
    return pl.pallas_call(
        attend_back_kernel,
        name="attend_back",
        grid=(pairs, rows),
        in_specs=[
            pair_block, pair_block, pair_block,
            pl.BlockSpec((1, 2, 2, 256, 384), lambda p, r: (r, p, 0, 0, 0)), pair_block,
            whole(comb_q.shape), whole(comb_k.shape),
            row_block(LANES), row_block(LANES), row_block(LANES),
        ],
        out_specs=[pair_block, pair_block, pair_block, whole(gp_shape)],
        out_shape=[slab, slab, slab, jax.ShapeDtypeStruct(gp_shape, jnp.float32)],
        compiler_params=pltpu.CompilerParams(vmem_limit_bytes=48 << 20),
    )(q, k, v, probs, dctx, comb_q, comb_k, *feats)


def pos_grad(gp):
    own = gp[:, 0, :HD] + gp[:, 1, HD:]
    even, odd = own[:, :, : PE // 2], own[:, :, LANES : LANES + PE // 2]
    return jnp.stack([even, odd], axis=-1).reshape(2, HD, PE).transpose(0, 2, 1).reshape(-1)


TILE = 256
FF_BLOCK = 768
ROOT_HALF = math.sqrt(0.5)
ROOT_TWO_PI = 1.0 / math.sqrt(2.0 * math.pi)


def normed(values):
    offset = values - jnp.mean(values, axis=1, keepdims=True)
    inverse = lax.rsqrt(jnp.mean(offset * offset, axis=1, keepdims=True) + norm_eps)
    return offset * inverse, inverse


def normed_back(grad, normal, inverse):
    return inverse * (
        grad
        - jnp.mean(grad, axis=1, keepdims=True)
        - normal * jnp.mean(grad * normal, axis=1, keepdims=True)
    )


def middle_kernel(
    x_ref, ctx_ref, cot_ref, w_out_ref, w_up_ref, w_down_ref, vec_ref, b_up_ref,
    out_ref, act_ref, h_ref, dffn_ref, dup_ref, dattn_ref, dz1_ref, dctx_ref, sums_ref, sum_up_ref,
    slope_ref,
):
    @pl.when(pl.program_id(0) == 0)
    def _():
        sums_ref[...] = jnp.zeros_like(sums_ref)
        sum_up_ref[...] = jnp.zeros_like(sum_up_ref)

    f32, bf16 = jnp.float32, jnp.bfloat16
    vec = vec_ref[...].astype(f32)
    b_out, gain1, shift1, b_down, gain2, shift2 = (vec[i : i + 1] for i in range(6))
    z1 = x_ref[...].astype(f32) + mm(ctx_ref[...], w_out_ref[...]) + b_out
    n1, r1 = normed(z1)
    h = n1 * gain1 + shift1
    h_low = h.astype(bf16)
    h_ref[...] = h_low
    z2 = h + b_down
    hidden = w_up_ref.shape[1]
    for j in range(0, hidden, FF_BLOCK):
        at = slice(j, j + FF_BLOCK)
        up = mm(h_low, w_up_ref[:, at]) + b_up_ref[:, at].astype(f32)
        phi = 0.5 * (1.0 + lax.erf(up * ROOT_HALF))
        slope_ref[:, at] = phi + up * (ROOT_TWO_PI * jnp.exp(-0.5 * up * up))
        act = (up * phi).astype(bf16)
        act_ref[:, at] = act
        z2 = z2 + mm(act, w_down_ref[at, :])
    n2, r2 = normed(z2)
    out_ref[...] = (n2 * gain2 + shift2).astype(bf16)
    g = cot_ref[...].astype(f32)
    dz2 = normed_back(g * gain2, n2, r2)
    dffn = dz2.astype(bf16)
    dffn_ref[...] = dffn
    dh = dz2
    for j in range(0, hidden, FF_BLOCK):
        at = slice(j, j + FF_BLOCK)
        dup = (mm_nt(dffn, w_down_ref[at, :]) * slope_ref[:, at]).astype(bf16)
        dup_ref[:, at] = dup
        sum_up_ref[:, at] += jnp.sum(dup.astype(f32), axis=0, keepdims=True)
        dh = dh + mm_nt(dup, w_up_ref[:, at])
    dz1 = normed_back(dh * gain1, n1, r1)
    dattn = dz1.astype(bf16)
    dz1_ref[...] = dz1
    dattn_ref[...] = dattn
    dctx_ref[...] = mm_nt(dattn, w_out_ref[...]).astype(bf16)
    for i, v in enumerate((dattn.astype(f32), dh * n1, dh, dffn.astype(f32), g * n2, g)):
        sums_ref[i : i + 1, :] += jnp.sum(v, axis=0, keepdims=True)


def middle(x, ctx, cot, w_out, w_up, w_down, vecs, b_up):
    tokens, width = x.shape
    hidden = w_up.shape[1]
    tile = lambda w: pl.BlockSpec((TILE, w), lambda i: (i, 0))
    whole = lambda s: pl.BlockSpec(s, lambda i: (0,) * len(s), pipeline_mode=pl.Buffered(1))
    out = lambda w, t=jnp.bfloat16: jax.ShapeDtypeStruct((tokens, w), t)
    return pl.pallas_call(
        middle_kernel,
        name="middle",
        grid=(tokens // TILE,),
        in_specs=[
            tile(width), tile(width), tile(width), whole(w_out.shape), whole(w_up.shape),
            whole(w_down.shape), whole(vecs.shape), whole(b_up.shape),
        ],
        out_specs=[
            tile(width), tile(hidden), tile(width), tile(width), tile(hidden), tile(width),
            tile(width), tile(width),
            pl.BlockSpec((8, width), lambda i: (0, 0)), pl.BlockSpec((1, hidden), lambda i: (0, 0)),
        ],
        out_shape=[
            out(width), out(hidden), out(width), out(width), out(hidden), out(width),
            out(width, jnp.float32), out(width),
            jax.ShapeDtypeStruct((8, width), jnp.float32), jax.ShapeDtypeStruct((1, hidden), jnp.float32),
        ],
        scratch_shapes=[pltpu.VMEM((TILE, hidden), jnp.float32)],
        compiler_params=pltpu.CompilerParams(vmem_limit_bytes=58 << 20),
    )(x, ctx, cot, w_out, w_up, w_down, vecs, b_up)


def body(
    tokens, page_ids, box_coords, w_qkv, b_qkv, w_pos, w_out, b_out, gain_one, shift_one,
    w_up, b_up, w_down, b_down, gain_two, shift_two, cotangent,
):
    width = tokens.shape[-1]
    x = tokens.reshape(-1, width)
    devices = lax.axis_size("fsdp")
    small = (b_qkv, w_pos, b_up, b_out, gain_one, shift_one, b_down, gain_two, shift_two)
    sizes = [s.shape[0] for s in small]
    packed = lax.all_gather(jnp.concatenate(small), "fsdp", axis=0)
    pieces, at = [], 0
    for size in sizes:
        pieces.append(packed[:, at : at + size].reshape(-1))
        at += size
    f_b_qkv, f_pos, f_b_up = pieces[:3]
    vecs = jnp.pad(jnp.stack(pieces[3:]), ((0, 2), (0, 0)))
    f_qkv, f_out, f_up, f_down = (
        lax.all_gather(s, "fsdp", axis=0, tiled=True) for s in (w_qkv, w_out, w_up, w_down)
    )
    pos = f_pos.reshape(2, PE, HD)
    comb_q, comb_k = comb_weights(pos[1]), comb_weights(pos[0])
    feats = features(box_coords)
    q, k, v, ctx, probs = attend(x, f_qkv, f_b_qkv, comb_q, comb_k, feats, page_ids)
    cot = cotangent.reshape(-1, width)
    out, act, h_low, dffn, dup, dattn, dz1, dctx, sums, sum_up = middle(
        x, ctx, cot, f_out, f_up, f_down, vecs, f_b_up.reshape(1, -1)
    )

    def total(a, b):
        part = lax.dot_general(
            a, b, (((0,), (0,)), ((), ())), preferred_element_type=jnp.float32
        ).astype(jnp.bfloat16)
        mine = lax.psum_scatter(part, "fsdp", scatter_dimension=0, tiled=True)
        return lax.psum(mine, "rep").astype(jnp.float32)

    g_down, g_up, g_out = total(act, dffn), total(h_low, dup), total(ctx, dattn)
    dq, dk, dv, gp = attend_back(q, k, v, probs, dctx, comb_q, comb_k, feats)
    dqkv = jnp.concatenate([dq, dk, dv], axis=1)
    g_qkv = total(x, dqkv)
    grad_x = dz1 + lax.dot_general(
        dqkv, f_qkv, (((1,), (1,)), ((), ())), preferred_element_type=jnp.float32
    )
    sum_qkv = jnp.sum(dqkv.astype(jnp.float32), axis=0)
    vectors = (sum_qkv, pos_grad(gp), sum_up[0]) + tuple(sums[i] for i in range(6))
    flat = jnp.concatenate([g.reshape(devices, -1) for g in vectors], axis=1)
    summed = lax.psum(lax.psum_scatter(flat, "fsdp", scatter_dimension=0, tiled=True), "rep")[0]
    outs, at = [], 0
    for size in sizes:
        outs.append(summed[at : at + size])
        at += size
    g_b_qkv, g_pos, g_b_up, g_b_out, g_gain1, g_shift1, g_b_down, g_gain2, g_shift2 = outs
    return (
        out.reshape(tokens.shape), grad_x.astype(jnp.bfloat16).reshape(tokens.shape),
        g_qkv, g_b_qkv, g_pos, g_out, g_b_out, g_gain1, g_shift1,
        g_up, g_b_up, g_down, g_b_down, g_gain2, g_shift2,
    )


def solution(mesh):
    in_specs = (
        P(("fsdp", "rep"), None, None),
        P(("fsdp", "rep"), None),
        P(None, ("fsdp", "rep"), None),
        P("fsdp", None),
        P("fsdp"),
        P("fsdp"),
        P("fsdp", None),
        P("fsdp"),
        P("fsdp"),
        P("fsdp"),
        P("fsdp", None),
        P("fsdp"),
        P("fsdp", None),
        P("fsdp"),
        P("fsdp"),
        P("fsdp"),
        P(("fsdp", "rep"), None, None),
    )
    out_specs = (
        P(("fsdp", "rep"), None, None),
        P(("fsdp", "rep"), None, None),
        P("fsdp", None),
        P("fsdp"),
        P("fsdp"),
        P("fsdp", None),
        P("fsdp"),
        P("fsdp"),
        P("fsdp"),
        P("fsdp", None),
        P("fsdp"),
        P("fsdp", None),
        P("fsdp"),
        P("fsdp"),
        P("fsdp"),
    )
    return jax.shard_map(body, mesh=mesh, in_specs=in_specs, out_specs=out_specs, check_vma=False)
```
